32 devices in a mesh: section: 2 (over y), seq: 4 (over x, core), rep: 4 (over z).
Axes of the slice: x: 2, y: 2, z: 4, core: 2. Of those that a mesh axis runs over, the one named last changes fastest.
Arguments:
- inputs: bfloat16 [2, 4, 512, 1152], P(None, 'rep', 'seq', 'section'), may hold values from -6 to 6
- w_query: bfloat16 [2, 1152, 1152], P('section', 'seq'), may hold values from -0.1875 to 0.1875
- w_key: bfloat16 [2, 1152, 384], P('section', 'seq'), may hold values from -0.1875 to 0.1875
- w_value: bfloat16 [2, 1152, 384], P('section', 'seq'), may hold values from -0.1875 to 0.1875
- w_out: bfloat16 [2, 1152, 1152], P('section', 'seq'), may hold values from -1.5 to 1.5
- w_gate: bfloat16 [2, 1152, 3072], P('section', 'seq'), may hold values from -0.1875 to 0.1875
- w_up: bfloat16 [2, 1152, 3072], P('section', 'seq'), may hold values from -0.1875 to 0.1875
- w_down: bfloat16 [2, 3072, 1152], P('section', 'seq'), may hold values from -0.109375 to 0.109375
- norm_attn: bfloat16 [2, 1152], P('section', 'seq'), may hold values from 0.5 to 1.5
- norm_ffn: bfloat16 [2, 1152], P('section', 'seq'), may hold values from 0.5 to 1.5
- image_start: int32 [2, 4], P(None, 'rep'), may hold values from 0 to 256, as said below
- cotangent: bfloat16 [2, 4, 512, 1152], P(None, 'rep', 'seq', 'section'), may hold values from -6 to 6
Outputs:
- block_out: float32 [2, 4, 512, 1152], P(None, 'rep', 'seq', 'section')
- input_grad: float32 [2, 4, 512, 1152], P(None, 'rep', 'seq', 'section')
- grad_query: float32 [2, 1152, 1152], P('section', 'seq')
- grad_key: float32 [2, 1152, 384], P('section', 'seq')
- grad_value: float32 [2, 1152, 384], P('section', 'seq')
- grad_out: float32 [2, 1152, 1152], P('section', 'seq')
- grad_gate: float32 [2, 1152, 3072], P('section', 'seq')
- grad_up: float32 [2, 1152, 3072], P('section', 'seq')
- grad_down: float32 [2, 3072, 1152], P('section', 'seq')
- grad_norm_attn: float32 [2, 1152], P('section', 'seq')
- grad_norm_ffn: float32 [2, 1152], P('section', 'seq')
The draws below stay inside these ranges and needn't reach their ends.
Inputs may be any that keep to these rules, and one draw needn't show every extreme that they name: `image_start`: each sequence's image span starts at a multiple of 256 and lies inside the sequence.
All inputs are finite; a program needn't handle non-finite values.
Results may differ from the reference program's by a relative error of at most 0.025.
Values may be sent and summed in bfloat16 or wider, within the bound.
No kernel may reach another device: no remote copies, remote signals or barrier semaphores. Data moves between devices by JAX's collectives and lax.ppermute only.
A program may use at most 256 MiB of HBM per device.

```python
import jax
import jax.numpy as jnp
from jax import lax

D = 1152
HQ = 18
KVH = 6
DH = 64
FF = 3072
MICRO = 2
IMG = 256
LENGTH = 512
SEQS = 4
N_SECTION = 2


def draw_image_start(key, part):
    count = LENGTH // IMG
    raw_index = jax.random.randint(key, (MICRO, SEQS), 0, count)
    raw_index = raw_index.at[0, 0].set(0).at[MICRO - 1, SEQS - 1].set(count - 1)
    return (raw_index * IMG).astype(jnp.int32)


def level_of(key, extent, cuts, low, largest):
    loudness = 1.0
    for dim, shards_of in cuts:
        steps = jax.random.uniform(jax.random.fold_in(jax.random.fold_in(key, 6), dim), (shards_of,), jnp.float32, low / len(cuts), largest / len(cuts))
        loudness = loudness * jnp.repeat(jnp.exp(steps), extent[dim] // shards_of).reshape((-1,) + (1,) * (len(extent) - 1 - dim))
    return loudness


def noise(rng, extent, scale, bound, cuts=(), kind=jnp.bfloat16):
    loudness = level_of(rng, extent, cuts, -0.22, 0.18) if cuts else 1.0
    values = jax.random.normal(rng, extent, jnp.float32) * scale * loudness
    return jnp.minimum(jnp.maximum(values, -bound), bound).astype(kind)


def setup_inputs(seed: int = 0) -> dict:
    key_of = jax.random.split(jax.random.key(seed), 13)
    inputs = noise(key_of[0], (MICRO, SEQS, LENGTH, D), 1.0, 6.0, ((1, 4), (2, 4), (3, 2)))
    w_query = noise(key_of[1], (N_SECTION, D, HQ * DH), D ** -0.5, 0.1875, ((0, 2), (1, 4)))
    w_key = noise(key_of[2], (N_SECTION, D, KVH * DH), D ** -0.5, 0.1875, ((0, 2), (1, 4)))
    w_value = noise(key_of[3], (N_SECTION, D, KVH * DH), D ** -0.5, 0.1875, ((0, 2), (1, 4)))
    w_out = noise(key_of[4], (N_SECTION, HQ * DH, D), (max(1, HQ * DH * 8 // LENGTH)) ** -0.5, 1.5, ((0, 2), (1, 4)))
    w_gate = noise(key_of[5], (N_SECTION, D, FF), D ** -0.5, 0.1875, ((0, 2), (1, 4)))
    w_up = noise(key_of[6], (N_SECTION, D, FF), D ** -0.5, 0.1875, ((0, 2), (1, 4)))
    w_down = noise(key_of[7], (N_SECTION, FF, D), FF ** -0.5, 0.109375, ((0, 2), (1, 4)))
    norm_attn = jnp.clip(1.0 + 0.1 * jax.random.normal(key_of[8], (N_SECTION, D), jnp.float32), 0.5, 1.5).astype(jnp.bfloat16)
    norm_ffn = jnp.clip(1.0 + 0.1 * jax.random.normal(key_of[9], (N_SECTION, D), jnp.float32), 0.5, 1.5).astype(jnp.bfloat16)
    image_start = draw_image_start(jax.random.fold_in(key_of[12], 71), 0)
    cotangent = noise(key_of[11], (MICRO, SEQS, LENGTH, D), 1.0, 6.0, ((1, 4), (2, 4), (3, 2)))
    return {"inputs": inputs, "w_query": w_query, "w_key": w_key, "w_value": w_value, "w_out": w_out, "w_gate": w_gate, "w_up": w_up, "w_down": w_down, "norm_attn": norm_attn, "norm_ffn": norm_ffn, "image_start": image_start, "cotangent": cotangent}


@jax.custom_vjp
def low(v):
    return lax.optimization_barrier(v.astype(jnp.bfloat16)).astype(jnp.float32)

@jax.custom_vjp
def low_back(v):
    return v

def low_keep(v):
    return (low(v), None)

def low_pass(kept, grad):
    return (grad,)

def back_keep(v):
    return (v, None)

def back_low(kept, grad):
    return (low(grad),)
low.defvjp(low_keep, low_pass)
low_back.defvjp(back_keep, back_low)
masked_value = -1e+30

def matmul(left, right):
    return jnp.dot(left, right, precision=lax.Precision.HIGHEST, preferred_element_type=jnp.float32)

def rms_norm(hidden, gain):
    return hidden * lax.rsqrt(lax.optimization_barrier(jnp.mean(hidden * hidden, axis=-1, keepdims=True)) + 1e-05) * gain

def tables(positions):
    frequency = 10000.0 ** (-jnp.arange(DH // 2, dtype=jnp.float32) / (DH // 2))
    angles = positions.astype(jnp.float32)[:, None] * frequency[None, :]
    return (jnp.cos(angles)[:, None, :], jnp.sin(angles)[:, None, :])

def rotate(tensor, cosine, sine_table):
    half_width = tensor.shape[-1] // 2
    leading = tensor[..., :half_width]
    trailing = tensor[..., half_width:]
    return jnp.concatenate([leading * cosine - trailing * sine_table, trailing * cosine + leading * sine_table], axis=-1)

def one_layer(hidden, weights, span_start):
    w_query, w_key, w_value, w_out, w_gate, w_up, w_down, gain_attn, gain_ffn = weights
    length = hidden.shape[0]
    group_size = HQ // KVH
    positions = jnp.arange(length, dtype=jnp.int32)
    cosine, sine_table = tables(positions)
    normed = low(rms_norm(hidden, gain_attn))
    queries = low(rotate(low_back(matmul(normed, w_query)).reshape(length, HQ, DH), cosine, sine_table))
    keys = low(rotate(low_back(matmul(normed, w_key)).reshape(length, KVH, DH), cosine, sine_table))
    values = low(low_back(matmul(normed, w_value))).reshape(length, KVH, DH)
    grouped = queries.reshape(length, KVH, group_size, DH)
    scores = low_back(jnp.einsum('qkgd,lkd->kgql', grouped, keys, precision=lax.Precision.HIGHEST))
    inside = (positions >= span_start) & (positions < span_start + IMG)
    allowed = (positions[None, :] <= positions[:, None]) | inside[:, None] & inside[None, :]
    logits = jnp.where(allowed, scores * DH ** (-0.5), masked_value)
    attend = low(jax.nn.softmax(logits, axis=-1))
    mixed = jnp.einsum('kgql,lkd->qkgd', attend, values, precision=lax.Precision.HIGHEST).reshape(length, HQ * DH)
    mixed = low_back(low(mixed))
    middle = hidden + low_back(matmul(mixed, w_out))
    normed_ffn = low(rms_norm(middle, gain_ffn))
    gate_proj = low_back(matmul(normed_ffn, w_gate))
    up_proj = low_back(matmul(normed_ffn, w_up))
    inner = low(jax.nn.silu(gate_proj) * up_proj)
    return middle + low_back(matmul(inner, w_down))

def two_layers(sequence, span_start, weights):
    hidden = sequence
    for layer_index in range(N_SECTION):
        hidden = one_layer(hidden, tuple((matrix[layer_index] for matrix in weights)), span_start)
    return hidden

def forward(inputs, weights, image_start):
    flat = inputs.reshape((-1,) + inputs.shape[2:])
    starts = image_start.reshape(-1)
    checked = jax.checkpoint(two_layers)
    outputs = lax.map(lambda operands: checked(operands[0], operands[1], weights), (flat, starts))
    return outputs.reshape(inputs.shape)

def reference(inputs, w_query, w_key, w_value, w_out, w_gate, w_up, w_down, norm_attn, norm_ffn, image_start, cotangent):
    weights = (w_query.astype(jnp.float32), w_key.astype(jnp.float32), w_value.astype(jnp.float32), w_out.astype(jnp.float32), w_gate.astype(jnp.float32), w_up.astype(jnp.float32), w_down.astype(jnp.float32), norm_attn.astype(jnp.float32), norm_ffn.astype(jnp.float32))
    outputs, pull = jax.vjp(lambda source, params: forward(source, params, image_start), inputs.astype(jnp.float32), weights)
    source_grad, param_grads = pull(cotangent.astype(jnp.float32))
    return (outputs, source_grad, param_grads[0], param_grads[1], param_grads[2], param_grads[3], param_grads[4], param_grads[5], param_grads[6], param_grads[7], param_grads[8])
```

```python
import functools

import jax
import jax.numpy as jnp
from jax import lax
from jax.experimental import pallas as pl
from jax.experimental.pallas import tpu as pltpu
from jax.sharding import PartitionSpec as P

HQ = 18
KVH = 6
DH = 64
IMG = 256
GROUP = HQ // KVH
PAIRS = KVH // 2
QT = 2 * GROUP * DH
KT = 2 * DH
masked_value = -1e30
F32 = jnp.float32
BF16 = jnp.bfloat16


def flip(block, bit, axis="seq"):
    count = lax.axis_size(axis)
    return lax.ppermute(block, axis, [(i, i ^ bit) for i in range(count)])


def shifted(block, axis, distance):
    devices = range(lax.axis_size(axis))
    route = [(i - distance, i) for i in devices if i - distance in devices]
    return lax.ppermute(block, axis, route)


def bits_below(count):
    return [1 << i for i in range(count.bit_length() - 1)]


def flip_gather(block, count):
    held = {0: block}
    for bit in reversed(bits_below(count)):
        held.update({p | bit: flip(piece, bit) for p, piece in list(held.items())})
    return [held[p] for p in range(count)]


def flip_reduce(pieces, count):
    held = dict(enumerate(pieces))
    for bit in bits_below(count):
        kept = [p for p in held if not p & bit]
        held = {p: held[p] + flip(held[p | bit].astype(BF16), bit).astype(F32) for p in kept}
    return held[0]


def gather_rows(shard, count, me):
    pieces = flip_gather(shard, count)
    whole = jnp.zeros((count,) + shard.shape, shard.dtype)
    for p, piece in enumerate(pieces):
        start = (me ^ p,) + (0,) * shard.ndim
        whole = lax.dynamic_update_slice(whole, piece[None], start)
    return whole.reshape((count * shard.shape[0],) + shard.shape[1:])


def rep_sum(value):
    count = lax.axis_size("rep")
    if count != 4:
        return lax.psum(value, "rep").astype(BF16)
    here = lax.axis_index("rep")
    inner = (here == 1) | (here == 2)
    arrived = lax.ppermute(value, "rep", [(0, 1), (3, 2)])
    value = value + arrived
    arrived = lax.ppermute(value, "rep", [(1, 2), (2, 1)])
    value = value + arrived
    arrived = lax.ppermute(value, "rep", [(1, 0), (2, 3)])
    return jnp.where(inner, value, arrived)


def other_half(tile):
    lane = lax.broadcasted_iota(jnp.int32, tile.shape, 1)
    low = lane % DH < DH // 2
    return jnp.where(low, pltpu.roll(tile, KT - DH // 2, 1), pltpu.roll(tile, DH // 2, 1))


def turn_kernel(x_ref, cos_ref, sin_ref, q_ref, kv_ref):
    cosine, sine = cos_ref[...], sin_ref[...]
    width_q, width_k = HQ * DH, KVH * DH
    for start in range(0, width_q, KT):
        tile = x_ref[:, start : start + KT]
        turned = tile * cosine + other_half(tile) * sine
        q_ref[:, start : start + KT] = (turned * DH ** (-0.5)).astype(BF16)
    for start in range(0, width_k, KT):
        tile = x_ref[:, width_q + start : width_q + start + KT]
        turned = tile * cosine + other_half(tile) * sine
        kv_ref[:, start : start + KT] = turned.astype(BF16)
    kv_ref[:, width_k:] = x_ref[:, width_q + width_k :].astype(BF16)


def turn(qkv, cosine, sine):
    rows = qkv.shape[0]
    return pl.pallas_call(
        turn_kernel,
        out_shape=(
            jax.ShapeDtypeStruct((rows, HQ * DH), BF16),
            jax.ShapeDtypeStruct((rows, 2 * KVH * DH), BF16),
        ),
        cost_estimate=pl.CostEstimate(
            flops=qkv.size * 6, bytes_accessed=qkv.size * 6, transcendentals=0
        ),
        name="turn",
    )(qkv, cosine, sine)


def turn_back_kernel(dk_ref, dv_ref, cos_ref, sin_ref, out_ref):
    cosine, sine = cos_ref[...], sin_ref[...]
    width_k = KVH * DH
    for start in range(0, width_k, KT):
        tile = dk_ref[:, start : start + KT]
        turned = tile * cosine - other_half(tile) * sine
        out_ref[:, start : start + KT] = turned.astype(BF16)
    out_ref[:, width_k:] = dv_ref[...].astype(BF16)


def turn_back(dk, dv, cosine, sine):
    rows = dk.shape[0]
    return pl.pallas_call(
        turn_back_kernel,
        out_shape=jax.ShapeDtypeStruct((rows, 2 * KVH * DH), BF16),
        cost_estimate=pl.CostEstimate(
            flops=dk.size * 6, bytes_accessed=dk.size * 12, transcendentals=0
        ),
        name="turn_back",
    )(dk, dv, cosine, sine)


def dot_nn(left, right):
    return jnp.dot(left, right, preferred_element_type=F32)


def attend_kernel(q_ref, k_ref, v_ref, bias_ref, o_ref, lse_ref):
    bias = bias_ref[...]
    values_t = v_ref[...].T
    for tile in range(GROUP):
        queries_t = q_ref[:, tile * KT : (tile + 1) * KT].T
        outs = []
        for half in range(2):
            head = 2 * tile + half
            kv = head // GROUP
            keys = k_ref[:, kv * DH : (kv + 1) * DH]
            logits = dot_nn(keys, queries_t[half * DH : (half + 1) * DH]) + bias
            top = jnp.max(logits, axis=0, keepdims=True)
            exponent = jnp.exp(logits - top)
            total = jnp.sum(exponent, axis=0, keepdims=True)
            attend = (exponent * (1.0 / total)).astype(BF16)
            outs.append(dot_nn(values_t[kv * DH : (kv + 1) * DH], attend))
            lse_ref[0, head : head + 1, :] = top + jnp.log(total)
        joined = jnp.concatenate(outs, axis=0).T
        o_ref[:, tile * KT : (tile + 1) * KT] = joined.astype(BF16)


def attend_forward(queries, keys_values, bias):
    rows, length = queries.shape[0], keys_values.shape[0]
    count = HQ * rows * length
    return pl.pallas_call(
        attend_kernel,
        grid=(PAIRS,),
        in_specs=[
            pl.BlockSpec((rows, QT), lambda i: (0, i)),
            pl.BlockSpec((length, KT), lambda i: (0, i)),
            pl.BlockSpec((length, KT), lambda i: (0, i + PAIRS)),
            pl.BlockSpec((length, rows), lambda i: (0, 0)),
        ],
        out_specs=[
            pl.BlockSpec((rows, QT), lambda i: (0, i)),
            pl.BlockSpec((1, 8, rows), lambda i: (i, 0, 0)),
        ],
        out_shape=(
            jax.ShapeDtypeStruct((rows, HQ * DH), BF16),
            jax.ShapeDtypeStruct((PAIRS, 8, rows), F32),
        ),
        cost_estimate=pl.CostEstimate(
            flops=count * 4 * DH, bytes_accessed=4 << 20, transcendentals=count
        ),
        name="attend",
    )(queries, keys_values, keys_values, bias)


def attend_back_kernel(
    q_ref, k_ref, v_ref, do_ref, bias_ref, lse_ref, cos_ref, sin_ref, dq_ref, dk_ref, dv_ref
):
    bias = bias_ref[...]
    keys_t = k_ref[...].T
    dk = [None, None]
    dv = [None, None]
    for tile in range(GROUP):
        q_tile = q_ref[:, tile * KT : (tile + 1) * KT]
        do_tile = do_ref[:, tile * KT : (tile + 1) * KT]
        queries_t = q_tile.T
        do_t = do_tile.T
        grads = []
        for half in range(2):
            head = 2 * tile + half
            kv = head // GROUP
            span = slice(half * DH, (half + 1) * DH)
            kv_span = slice(kv * DH, (kv + 1) * DH)
            logits = dot_nn(k_ref[:, kv_span], queries_t[span]) + bias
            attend = jnp.exp(logits - lse_ref[0, head : head + 1, :])
            d_attend = dot_nn(v_ref[:, kv_span], do_t[span])
            delta = jnp.sum(d_attend * attend, axis=0, keepdims=True)
            d_scores = (attend * (d_attend - delta)).astype(BF16)
            grads.append(dot_nn(keys_t[kv_span], d_scores))
            dk_term = dot_nn(d_scores, q_tile[:, span])
            dv_term = dot_nn(attend.astype(BF16), do_tile[:, span])
            dk[kv] = dk_term if dk[kv] is None else dk[kv] + dk_term
            dv[kv] = dv_term if dv[kv] is None else dv[kv] + dv_term
        joined = jnp.concatenate(grads, axis=0).T * DH ** (-0.5)
        turned = joined * cos_ref[...] - other_half(joined) * sin_ref[...]
        dq_ref[:, tile * KT : (tile + 1) * KT] = turned.astype(BF16)
    dk_ref[...] = jnp.concatenate(dk, axis=1)
    dv_ref[...] = jnp.concatenate(dv, axis=1)


def attend_backward(queries, keys_values, d_mixed, bias, lse, cosine, sine):
    rows, length = queries.shape[0], keys_values.shape[0]
    count = HQ * rows * length
    return pl.pallas_call(
        attend_back_kernel,
        grid=(PAIRS,),
        in_specs=[
            pl.BlockSpec((rows, QT), lambda i: (0, i)),
            pl.BlockSpec((length, KT), lambda i: (0, i)),
            pl.BlockSpec((length, KT), lambda i: (0, i + PAIRS)),
            pl.BlockSpec((rows, QT), lambda i: (0, i)),
            pl.BlockSpec((length, rows), lambda i: (0, 0)),
            pl.BlockSpec((1, 8, rows), lambda i: (i, 0, 0)),
            pl.BlockSpec((rows, KT), lambda i: (0, 0)),
            pl.BlockSpec((rows, KT), lambda i: (0, 0)),
        ],
        out_specs=[
            pl.BlockSpec((rows, QT), lambda i: (0, i)),
            pl.BlockSpec((length, KT), lambda i: (0, i)),
            pl.BlockSpec((length, KT), lambda i: (0, i)),
        ],
        out_shape=(
            jax.ShapeDtypeStruct((rows, HQ * DH), BF16),
            jax.ShapeDtypeStruct((length, KVH * DH), F32),
            jax.ShapeDtypeStruct((length, KVH * DH), F32),
        ),
        cost_estimate=pl.CostEstimate(
            flops=count * 10 * DH, bytes_accessed=8 << 20, transcendentals=count
        ),
        name="attend_back",
    )(queries, keys_values, keys_values, d_mixed, bias, lse, cosine, sine)


def dot_nt(left, right):
    return lax.dot_general(left, right, (((1,), (1,)), ((), ())), preferred_element_type=F32)


def inverse_rms(hidden):
    return lax.rsqrt(jnp.mean(hidden * hidden, axis=-1, keepdims=True) + 1e-05)


def forward_layer(hidden, weights, place):
    w_qkv, w_out, w_gu, w_down, gain_attn, gain_ffn = weights
    group, cosine, sine, bias = place
    rows = hidden.shape[0]
    normed = (hidden * inverse_rms(hidden) * gain_attn).astype(BF16)
    queries, kv_own = turn(dot_nn(normed, w_qkv), cosine, sine)
    kv_all = jnp.concatenate(flip_gather(kv_own, group), axis=0)
    mixed, lse = attend_forward(queries, kv_all, bias)
    middle = hidden + dot_nn(mixed, w_out)
    ffn_in = (middle * inverse_rms(middle) * gain_ffn).astype(BF16)
    gate_up = dot_nn(ffn_in, w_gu)
    width = gate_up.shape[1] // 2
    inner = (jax.nn.silu(gate_up[:, :width]) * gate_up[:, width:]).astype(BF16)
    out = middle + dot_nn(inner, w_down)
    return out, (hidden, normed, queries, kv_all, lse, mixed, middle, ffn_in, gate_up, inner)


def norm_back(hidden, gain, d_normed):
    inverse = inverse_rms(hidden)
    scaled = d_normed * gain
    back = inverse * (
        scaled
        - hidden * (inverse * inverse) * jnp.mean(scaled * hidden, axis=-1, keepdims=True)
    )
    return back, jnp.sum(d_normed * hidden * inverse, axis=0)


def backward_layer(out_grad, kept, weights, place):
    w_qkv, w_out, w_gu, w_down, gain_attn, gain_ffn = weights
    group, cosine, sine, bias = place
    hidden, normed, queries, kv_all, lse, mixed, middle, ffn_in, gate_up, inner = kept
    rows = hidden.shape[0]
    grad_low = out_grad.astype(BF16)
    d_inner = dot_nt(grad_low, w_down)
    width = gate_up.shape[1] // 2
    gate, up = gate_up[:, :width], gate_up[:, width:]
    sig = jax.nn.sigmoid(gate)
    d_gate = (d_inner * up * (sig * (1.0 + gate * (1.0 - sig)))).astype(BF16)
    d_up = (d_inner * (gate * sig)).astype(BF16)
    d_gu = jnp.concatenate([d_gate, d_up], axis=1)
    d_ffn_in = dot_nt(d_gu, w_gu)
    middle_back, gain_ffn_grad = norm_back(middle, gain_ffn, d_ffn_in)
    d_middle = out_grad + middle_back
    middle_low = d_middle.astype(BF16)
    d_mixed = dot_nt(middle_low, w_out).astype(BF16)
    d_q, dk_all, dv_all = attend_backward(
        queries, kv_all, d_mixed, bias, lse, cosine, sine
    )
    dk = flip_reduce([dk_all[p * rows : (p + 1) * rows] for p in range(group)], group)
    dv = flip_reduce([dv_all[p * rows : (p + 1) * rows] for p in range(group)], group)
    d_kv = turn_back(dk, dv, cosine, sine)
    d_qkv = jnp.concatenate([d_q, d_kv], axis=1)
    d_normed = dot_nt(d_qkv, w_qkv)
    hidden_back, gain_attn_grad = norm_back(hidden, gain_attn, d_normed)
    pairs = ((inner, grad_low), (ffn_in, d_gu), (mixed, middle_low), (normed, d_qkv))
    return d_middle + hidden_back, pairs, (gain_attn_grad, gain_ffn_grad)


def weight_grad(left, right, me, count, group):
    left_t = left.T
    depth = left_t.shape[0] // count

    def rows_of(p):
        first = lax.dynamic_slice_in_dim(left_t, (me ^ p) * depth, depth, 0)
        second = lax.dynamic_slice_in_dim(left_t, (me ^ p ^ group) * depth, depth, 0)
        return jnp.concatenate([first, second], axis=0)

    lefts = [rows_of(0)] + [flip(rows_of(p), p) for p in range(1, group)]
    rights = [right] + [flip(right, p) for p in range(1, group)]
    product = dot_nn(jnp.concatenate(lefts, axis=1), jnp.concatenate(rights, axis=0))
    sent = flip(product[depth:].astype(BF16), group)
    return rep_sum((product[:depth] + sent.astype(F32)).astype(BF16))


def shards(
    inputs,
    w_query,
    w_key,
    w_value,
    w_out,
    w_gate,
    w_up,
    w_down,
    norm_attn,
    norm_ffn,
    image_start,
    cotangent,
):
    is_first = lax.axis_index("section") == 0
    me = lax.axis_index("seq")
    count = lax.axis_size("seq")
    micro_count, _, piece_rows, half_width = inputs.shape
    group = count // micro_count
    length = piece_rows * count
    micro = me // group
    own_input = inputs[:, 0]
    own_cotan = cotangent[:, 0]
    incoming = flip(jnp.where(is_first, own_cotan, own_input), 1, "section")
    whole = jnp.where(
        is_first,
        jnp.concatenate([own_input, incoming], axis=-1),
        jnp.concatenate([incoming, own_cotan], axis=-1),
    )
    kept_block = lax.dynamic_index_in_dim(whole, micro, 0, keepdims=False)
    sent_block = lax.dynamic_index_in_dim(whole, 1 - micro, 0, keepdims=False)
    given = jnp.concatenate([kept_block, flip(sent_block, group)], axis=0).astype(F32)

    def positions(device):
        within = jnp.arange(piece_rows, dtype=jnp.int32)
        return jnp.concatenate(
            [device * piece_rows + within, (device ^ group) * piece_rows + within]
        )

    query_pos = positions(me)
    key_pos = jnp.concatenate([positions(me ^ p) for p in range(group)])
    start = lax.dynamic_index_in_dim(image_start[:, 0], micro, 0, keepdims=False)
    query_in = (query_pos >= start) & (query_pos < start + IMG)
    key_in = (key_pos >= start) & (key_pos < start + IMG)
    allowed = (key_pos[:, None] <= query_pos[None, :]) | (key_in[:, None] & query_in[None, :])
    bias = jnp.where(allowed, 0.0, masked_value).astype(F32)
    frequency = 10000.0 ** (-jnp.arange(DH // 2, dtype=F32) / (DH // 2))
    angles = query_pos.astype(F32)[:, None] * frequency[None, :]
    cosine = jnp.tile(jnp.cos(angles), (1, 4))
    sine = jnp.sin(angles)
    sine = jnp.concatenate([-sine, sine, -sine, sine], axis=1)
    place = (group, cosine, sine, bias)

    gains = flip_gather(jnp.stack([norm_attn[0], norm_ffn[0]]), count)
    gain_rows = jnp.zeros((count,) + gains[0].shape, BF16)
    for p, piece in enumerate(gains):
        gain_rows = lax.dynamic_update_slice(gain_rows, piece[None], (me ^ p, 0, 0))
    gain_rows = gain_rows.transpose(1, 0, 2).reshape(2, -1).astype(F32)
    qkv_shard = jnp.concatenate([w_query[0], w_key[0], w_value[0]], axis=1)
    gu_shard = jnp.concatenate([w_gate[0], w_up[0]], axis=1)
    weights = (
        gather_rows(qkv_shard, count, me),
        gather_rows(w_out[0], count, me),
        gather_rows(gu_shard, count, me),
        gather_rows(w_down[0], count, me),
        gain_rows[0],
        gain_rows[1],
    )

    first_out, _ = forward_layer(given, weights, place)
    received = shifted(first_out.astype(BF16), "section", 1).astype(F32)
    layer_in = jnp.where(is_first, given, received)
    block, kept = forward_layer(layer_in, weights, place)
    second_grad, _, _ = backward_layer(given, kept, weights, place)
    received = shifted(second_grad.astype(BF16), "section", -1).astype(F32)
    out_grad = jnp.where(is_first, received, given)
    first_grad, pairs, gain_grads = backward_layer(out_grad, kept, weights, place)

    down, gate_up, out, qkv = [weight_grad(*pair, me, count, group) for pair in pairs]
    gain_sums = lax.psum(jnp.stack(gain_grads), ("seq", "rep"))
    depth = gain_sums.shape[1] // count
    gain_sums = lax.dynamic_slice_in_dim(gain_sums, me * depth, depth, 1)

    def placed(result, from_first):
        kept_rows, sent_rows = result[:piece_rows], result[piece_rows:]
        back = flip(sent_rows.astype(BF16), group).astype(F32)
        first = jnp.where(micro == 0, kept_rows, back)
        second = jnp.where(micro == 0, back, kept_rows)
        rows = jnp.stack([first, second])
        low, high = rows[..., :half_width], rows[..., half_width:]
        if from_first:
            return jnp.where(is_first, low, shifted(high.astype(BF16), "section", 1).astype(F32))
        return jnp.where(is_first, shifted(low.astype(BF16), "section", -1).astype(F32), high)

    block_out = placed(block, False)[:, None]
    input_grad = placed(first_grad, True)[:, None]
    width = gate_up.shape[1] // 2
    wide, narrow = HQ * DH, KVH * DH
    wide_grads = [
        qkv[:, :wide],
        qkv[:, wide : wide + narrow],
        qkv[:, wide + narrow :],
        out,
        gate_up[:, :width],
        gate_up[:, width:],
        down,
        gain_sums[0],
        gain_sums[1],
    ]
    return (block_out, input_grad) + tuple(grad.astype(F32)[None] for grad in wide_grads)


def solution(mesh):
    rows = P("section", "seq", None)
    tokens = P(None, "rep", "seq", "section")
    in_specs = (tokens,) + (rows,) * 7 + (P("section", "seq"),) * 2 + (P(None, "rep"), tokens)
    out_specs = (tokens, tokens) + (rows,) * 7 + (P("section", "seq"),) * 2
    return jax.shard_map(shards, mesh=mesh, in_specs=in_specs, out_specs=out_specs, check_vma=False)
```

```python
import jax
import jax.numpy as jnp
from jax import lax
from jax.experimental import pallas as pl
from jax.experimental.pallas import tpu as pltpu
from jax.sharding import PartitionSpec as P

HQ = 18
KVH = 6
DH = 64
IMG = 256
GROUP = HQ // KVH
PAIRS = KVH // 2
QT = 2 * GROUP * DH
KT = 2 * DH
WQ = HQ * DH
WK = KVH * DH
masked_value = -1e30
F32 = jnp.float32
BF16 = jnp.bfloat16


def flip(block, bit, axis="seq"):
    return lax.ppermute(block, axis, [(i, i ^ bit) for i in range(lax.axis_size(axis))])


def shifted(block, axis, distance):
    devices = range(lax.axis_size(axis))
    route = [(i - distance, i) for i in devices if i - distance in devices]
    return lax.ppermute(block, axis, route)


def bits_below(count):
    return [1 << i for i in range(count.bit_length() - 1)]


def flip_gather(block, count):
    held = {0: block}
    for bit in reversed(bits_below(count)):
        held.update({p | bit: flip(piece, bit) for p, piece in list(held.items())})
    return [held[p] for p in range(count)]


def flip_reduce(pieces, count):
    held = dict(enumerate(pieces))
    for bit in bits_below(count):
        kept = [p for p in held if not p & bit]
        last = 2 * bit == count
        added = {p: flip(held[p | bit], bit) for p in kept}
        if last:
            return held[0], added[0]
        held = {p: held[p] + added[p] for p in kept}


def put_rows(pieces, places):
    whole = jnp.zeros((len(pieces),) + pieces[0].shape, pieces[0].dtype)
    for place, piece in zip(places, pieces):
        whole = lax.dynamic_update_slice(whole, piece[None], (place,) + (0,) * piece.ndim)
    return whole.reshape((len(pieces) * pieces[0].shape[0],) + pieces[0].shape[1:])


def gather_rows(shard, count, me):
    pieces = flip_gather(shard, count)
    return put_rows(pieces, [me ^ p for p in range(count)])


def gather_over_rep(shard, count, me):
    reps = lax.axis_size("rep")
    if count != 4 or shard.shape[0] % (8 * reps):
        return gather_rows(shard, count, me)
    here = lax.axis_index("rep")
    depth = shard.shape[0] // reps
    part = flip(lax.dynamic_slice_in_dim(shard, here * depth, depth, 0), 2)
    parts = [part] + [
        lax.ppermute(part, "rep", [(i, (i + k) % reps) for i in range(reps)])
        for k in range(1, reps)
    ]
    across = put_rows(parts, [(here - k) % reps for k in range(reps)])
    pieces = [shard, flip(shard, 1), across, flip(across, 1)]
    return put_rows(pieces, [me ^ p for p in range(count)])


def rep_sum(value):
    count = lax.axis_size("rep")
    if count != 4:
        return lax.psum(value, "rep").astype(BF16)
    here = lax.axis_index("rep")
    inner = (here == 1) | (here == 2)
    value = value + lax.ppermute(value, "rep", [(0, 1), (3, 2)])
    value = value + lax.ppermute(value, "rep", [(1, 2), (2, 1)])
    arrived = lax.ppermute(value, "rep", [(1, 0), (2, 3)])
    return jnp.where(inner, value, arrived)


def dot_nn(left, right):
    return jnp.dot(left, right, preferred_element_type=F32)


def dot_nt(left, right):
    return lax.dot_general(left, right, (((1,), (1,)), ((), ())), preferred_element_type=F32)


def inverse_rms(hidden):
    return lax.rsqrt(jnp.mean(hidden * hidden, axis=-1, keepdims=True) + 1e-05)


def kernel(body, flops, size, **options):
    cost = pl.CostEstimate(flops=flops, bytes_accessed=size, transcendentals=0)
    return pl.pallas_call(body, cost_estimate=cost, **options)


def shape_of(rows, cols, kind=BF16):
    return jax.ShapeDtypeStruct((rows, cols), kind)


def fixed(*extent):
    return pl.BlockSpec(extent, lambda *step: (0,) * len(extent))


def other_half(tile):
    lane = lax.broadcasted_iota(jnp.int32, tile.shape, 1)
    low = lane % DH < DH // 2
    return jnp.where(low, pltpu.roll(tile, KT - DH // 2, 1), pltpu.roll(tile, DH // 2, 1))


def project_kernel(h_ref, gain_ref, w_ref, cos_ref, sin_ref, normed_ref, q_ref, kv_ref):
    step = pl.program_id(0)

    @pl.when(step == 0)
    def _():
        hidden = h_ref[...].astype(F32)
        normed_ref[...] = (hidden * inverse_rms(hidden) * gain_ref[...]).astype(BF16)

    product = dot_nn(normed_ref[...], w_ref[...])

    def turned(scale, out_ref):
        for start in range(0, WK, KT):
            tile = product[:, start : start + KT]
            result = tile * cos_ref[...] + other_half(tile) * sin_ref[...]
            out_ref[:, start : start + KT] = (result * scale).astype(BF16)

    @pl.when(step < GROUP)
    def _():
        turned(DH ** (-0.5), q_ref)

    @pl.when(step == GROUP)
    def _():
        turned(1.0, kv_ref)

    @pl.when(step == GROUP + 1)
    def _():
        kv_ref[...] = product.astype(BF16)


def project(hidden, gain, w_qkv, cosine, sine):
    rows, model = hidden.shape
    return kernel(
        project_kernel,
        2 * rows * w_qkv.size,
        2 * w_qkv.size + 8 * hidden.size,
        grid=(GROUP + 2,),
        in_specs=[
            fixed(rows, model),
            fixed(1, model),
            pl.BlockSpec((model, WK), lambda j: (0, j)),
            fixed(rows, KT),
            fixed(rows, KT),
        ],
        out_specs=[
            fixed(rows, model),
            pl.BlockSpec((rows, WK), lambda j: (0, jnp.minimum(j, GROUP - 1))),
            pl.BlockSpec((rows, WK), lambda j: (0, jnp.maximum(j - GROUP, 0))),
        ],
        out_shape=(shape_of(rows, model), shape_of(rows, WQ), shape_of(rows, 2 * WK)),
    )(hidden, gain, w_qkv, cosine, sine)


def attend_kernel(q_ref, k_ref, v_ref, bias_ref, o_ref, lse_ref):
    bias = bias_ref[...]
    values_t = v_ref[...].T
    for tile in range(GROUP):
        queries_t = q_ref[:, tile * KT : (tile + 1) * KT].T
        outs = []
        for half in range(2):
            head = 2 * tile + half
            kv = head // GROUP
            keys = k_ref[:, kv * DH : (kv + 1) * DH]
            logits = dot_nn(keys, queries_t[half * DH : (half + 1) * DH]) + bias
            top = jnp.max(logits, axis=0, keepdims=True)
            exponent = jnp.exp(logits - top)
            total = jnp.sum(exponent, axis=0, keepdims=True)
            attend = (exponent * (1.0 / total)).astype(BF16)
            outs.append(dot_nn(values_t[kv * DH : (kv + 1) * DH], attend))
            lse_ref[0, head : head + 1, :] = top + jnp.log(total)
        joined = jnp.concatenate(outs, axis=0).T
        o_ref[:, tile * KT : (tile + 1) * KT] = joined.astype(BF16)


def attend_forward(queries, keys_values, bias):
    rows, length = queries.shape[0], keys_values.shape[0]
    count = HQ * rows * length
    return kernel(
        attend_kernel,
        count * 8 * DH,
        4 << 20,
        grid=(PAIRS,),
        in_specs=[
            pl.BlockSpec((rows, QT), lambda i: (0, i)),
            pl.BlockSpec((length, KT), lambda i: (0, i)),
            pl.BlockSpec((length, KT), lambda i: (0, i + PAIRS)),
            fixed(length, rows),
        ],
        out_specs=[
            pl.BlockSpec((rows, QT), lambda i: (0, i)),
            pl.BlockSpec((1, 8, rows), lambda i: (i, 0, 0)),
        ],
        out_shape=(shape_of(rows, WQ), jax.ShapeDtypeStruct((PAIRS, 8, rows), F32)),
    )(queries, keys_values, keys_values, bias)


def attend_back_kernel(
    q_ref, k_ref, v_ref, do_ref, bias_ref, lse_ref, cos_ref, sin_ref, dq_ref, *dkv_refs
):
    bias = bias_ref[...]
    keys_t = k_ref[...].T
    dk = [None, None]
    dv = [None, None]
    for tile in range(GROUP):
        q_tile = q_ref[:, tile * KT : (tile + 1) * KT]
        do_tile = do_ref[:, tile * KT : (tile + 1) * KT]
        queries_t = q_tile.T
        do_t = do_tile.T
        grads = []
        for half in range(2):
            head = 2 * tile + half
            kv = head // GROUP
            span = slice(half * DH, (half + 1) * DH)
            kv_span = slice(kv * DH, (kv + 1) * DH)
            logits = dot_nn(k_ref[:, kv_span], queries_t[span]) + bias
            attend = jnp.exp(logits - lse_ref[0, head : head + 1, :])
            d_attend = dot_nn(v_ref[:, kv_span], do_t[span])
            delta = jnp.sum(d_attend * attend, axis=0, keepdims=True)
            d_scores = (attend * (d_attend - delta)).astype(BF16)
            grads.append(dot_nn(keys_t[kv_span], d_scores))
            dk_term = dot_nn(d_scores, q_tile[:, span])
            dv_term = dot_nn(attend.astype(BF16), do_tile[:, span])
            dk[kv] = dk_term if dk[kv] is None else dk[kv] + dk_term
            dv[kv] = dv_term if dv[kv] is None else dv[kv] + dv_term
        joined = jnp.concatenate(grads, axis=0).T * DH ** (-0.5)
        turned = joined * cos_ref[...] - other_half(joined) * sin_ref[...]
        dq_ref[:, tile * KT : (tile + 1) * KT] = turned.astype(BF16)
    d_keys = jnp.concatenate(dk, axis=1).astype(BF16)
    d_values = jnp.concatenate(dv, axis=1).astype(BF16)
    rows = dq_ref.shape[0]
    for p in range(len(dkv_refs) // 2):
        dkv_refs[2 * p][...] = d_keys[p * rows : (p + 1) * rows]
        dkv_refs[2 * p + 1][...] = d_values[p * rows : (p + 1) * rows]


def attend_backward(queries, keys_values, d_mixed, bias, lse, cosine, sine):
    rows, length = queries.shape[0], keys_values.shape[0]
    count = HQ * rows * length
    narrow = pl.BlockSpec((rows, KT), lambda i: (0, i))
    total = 2 * (length // rows)
    return kernel(
        attend_back_kernel,
        count * 16 * DH,
        8 << 20,
        grid=(PAIRS,),
        in_specs=[
            pl.BlockSpec((rows, QT), lambda i: (0, i)),
            pl.BlockSpec((length, KT), lambda i: (0, i)),
            pl.BlockSpec((length, KT), lambda i: (0, i + PAIRS)),
            pl.BlockSpec((rows, QT), lambda i: (0, i)),
            fixed(length, rows),
            pl.BlockSpec((1, 8, rows), lambda i: (i, 0, 0)),
            fixed(rows, KT),
            fixed(rows, KT),
        ],
        out_specs=[pl.BlockSpec((rows, QT), lambda i: (0, i))] + [narrow] * total,
        out_shape=(shape_of(rows, WQ),) + (shape_of(rows, WK),) * total,
    )(queries, keys_values, keys_values, d_mixed, bias, lse, cosine, sine)


def mix_kernel(mixed_ref, w_ref, h_ref, gain_ref, middle_ref, ffn_ref):
    step = pl.program_id(0)

    @pl.when(step == 0)
    def _():
        middle_ref[...] = h_ref[...].astype(F32)

    middle_ref[...] += dot_nn(mixed_ref[...], w_ref[...])

    @pl.when(step == pl.num_programs(0) - 1)
    def _():
        middle = middle_ref[...]
        ffn_ref[...] = (middle * inverse_rms(middle) * gain_ref[...]).astype(BF16)


def mix(mixed, w_out, hidden, gain):
    rows, model = hidden.shape
    tile = WK
    return kernel(
        mix_kernel,
        2 * rows * w_out.size,
        2 * w_out.size + 8 * hidden.size,
        grid=(WQ // tile,),
        in_specs=[
            pl.BlockSpec((rows, tile), lambda j: (0, j)),
            pl.BlockSpec((tile, model), lambda j: (j, 0)),
            fixed(rows, model),
            fixed(1, model),
        ],
        out_specs=[fixed(rows, model), fixed(rows, model)],
        out_shape=(shape_of(rows, model, F32), shape_of(rows, model)),
    )(mixed, w_out, hidden, gain)


def gate_kernel(x_ref, wg_ref, wu_ref, inner_ref, *slope_refs):
    gate = dot_nn(x_ref[...], wg_ref[...])
    up = dot_nn(x_ref[...], wu_ref[...])
    sig = 1.0 / (1.0 + jnp.exp(-gate))
    silu = gate * sig
    inner_ref[...] = (silu * up).astype(BF16)
    if slope_refs:
        slope_refs[0][...] = (up * (sig * (1.0 + gate * (1.0 - sig)))).astype(BF16)
        slope_refs[1][...] = silu.astype(BF16)


def gate_up(ffn_in, w_gate, w_up, slopes):
    rows, model = ffn_in.shape
    width = w_gate.shape[1]
    tile = width // 4
    outs = 3 if slopes else 1
    cols = pl.BlockSpec((rows, tile), lambda j: (0, j))
    weight = pl.BlockSpec((model, tile), lambda j: (0, j))
    return kernel(
        gate_kernel,
        4 * rows * w_gate.size,
        4 * w_gate.size + 2 * outs * rows * width,
        grid=(width // tile,),
        in_specs=[fixed(rows, model), weight, weight],
        out_specs=[cols] * outs,
        out_shape=(shape_of(rows, width),) * outs,
    )(ffn_in, w_gate, w_up)


def down_kernel(inner_ref, w_ref, middle_ref, out_ref, low_ref):
    step = pl.program_id(0)

    @pl.when(step == 0)
    def _():
        out_ref[...] = middle_ref[...]

    out_ref[...] += dot_nn(inner_ref[...], w_ref[...])

    @pl.when(step == pl.num_programs(0) - 1)
    def _():
        low_ref[...] = out_ref[...].astype(BF16)


def down(inner, w_down, middle):
    rows, model = middle.shape
    width = w_down.shape[0]
    tile = width // 4
    return kernel(
        down_kernel,
        2 * rows * w_down.size,
        2 * w_down.size + 12 * middle.size,
        grid=(width // tile,),
        in_specs=[
            pl.BlockSpec((rows, tile), lambda j: (0, j)),
            pl.BlockSpec((tile, model), lambda j: (j, 0)),
            fixed(rows, model),
        ],
        out_specs=[fixed(rows, model), fixed(rows, model)],
        out_shape=(shape_of(rows, model, F32), shape_of(rows, model)),
    )(inner, w_down, middle)


def d_inner_kernel(g_ref, w_ref, gate_slope_ref, up_slope_ref, out_ref):
    d_inner = dot_nt(g_ref[...], w_ref[...])
    out_ref[0] = (d_inner * gate_slope_ref[...].astype(F32)).astype(BF16)
    out_ref[1] = (d_inner * up_slope_ref[...].astype(F32)).astype(BF16)


def d_inner(grad, w_down, gate_slope, up_slope):
    rows, model = grad.shape
    width = w_down.shape[0]
    tile = width // 4
    cols = pl.BlockSpec((rows, tile), lambda j: (0, j))
    return kernel(
        d_inner_kernel,
        2 * rows * w_down.size,
        2 * w_down.size + 8 * rows * width,
        grid=(width // tile,),
        in_specs=[
            fixed(rows, model),
            pl.BlockSpec((tile, model), lambda j: (j, 0)),
            cols,
            cols,
        ],
        out_specs=pl.BlockSpec((2, rows, tile), lambda j: (0, 0, j)),
        out_shape=jax.ShapeDtypeStruct((2, rows, width), BF16),
    )(grad, w_down, gate_slope, up_slope)


def norm_back(hidden, gain, d_normed):
    inverse = inverse_rms(hidden)
    scaled = d_normed * gain
    mean = jnp.mean(scaled * hidden, axis=-1, keepdims=True)
    back = inverse * (scaled - hidden * (inverse * inverse) * mean)
    return back, jnp.sum(d_normed * hidden * inverse, axis=0, keepdims=True)


def d_middle_kernel(
    d_ref, wg_ref, wu_ref, middle_ref, gain_ref, g_ref, wo_ref,
    dm_ref, low_ref, mixed_ref, gain_grad_ref, total,
):
    step = pl.program_id(0)
    half = pl.num_programs(0) // 2

    @pl.when(step == 0)
    def _():
        total[...] = jnp.zeros_like(total)

    @pl.when(step < half)
    def _():
        total[...] += dot_nt(d_ref[0], wg_ref[...])

    @pl.when(step >= half)
    def _():
        total[...] += dot_nt(d_ref[0], wu_ref[...])

    @pl.when(step == pl.num_programs(0) - 1)
    def _():
        back, gain_grad = norm_back(middle_ref[...], gain_ref[...], total[...])
        d_middle = g_ref[...].astype(F32) + back
        dm_ref[...] = d_middle
        low = d_middle.astype(BF16)
        low_ref[...] = low
        mixed_ref[...] = dot_nt(low, wo_ref[...]).astype(BF16)
        gain_grad_ref[...] = gain_grad


def d_middle(d_gu, w_gate, w_up, middle, gain, grad, w_out):
    rows, model = middle.shape
    width = w_gate.shape[1]
    tile = width // 2
    half = width // tile
    return kernel(
        d_middle_kernel,
        4 * rows * w_gate.size + 2 * rows * w_out.size,
        4 * w_gate.size + 4 * rows * width + 12 * middle.size,
        grid=(2 * half,),
        in_specs=[
            pl.BlockSpec((1, rows, tile), lambda j: (j // half, 0, j % half)),
            pl.BlockSpec((model, tile), lambda j: (0, jnp.minimum(j, half - 1))),
            pl.BlockSpec((model, tile), lambda j: (0, jnp.maximum(j - half, 0))),
            fixed(rows, model),
            fixed(1, model),
            fixed(rows, model),
            fixed(*w_out.shape),
        ],
        out_specs=[fixed(rows, model)] * 2 + [fixed(rows, WQ), fixed(1, model)],
        out_shape=(
            shape_of(rows, model, F32),
            shape_of(rows, model),
            shape_of(rows, WQ),
            shape_of(1, model, F32),
        ),
        scratch_shapes=[pltpu.VMEM((rows, model), F32)],
    )(d_gu, w_gate, w_up, middle, gain, grad, w_out)


def d_hidden_kernel(
    dq_ref, dk_ref, dv_ref, dk2_ref, dv2_ref, cos_ref, sin_ref, w_ref, h_ref, gain_ref, dm_ref,
    dkv_ref, dh_ref, low_ref, gain_grad_ref,
):
    for start in range(0, WK, KT):
        tile = dk_ref[:, start : start + KT].astype(F32)
        tile += dk2_ref[:, start : start + KT].astype(F32)
        turned = tile * cos_ref[...] - other_half(tile) * sin_ref[...]
        dkv_ref[:, start : start + KT] = turned.astype(BF16)
    dkv_ref[:, WK:] = (dv_ref[...].astype(F32) + dv2_ref[...].astype(F32)).astype(BF16)
    d_normed = dot_nt(dq_ref[...], w_ref[:, :WQ]) + dot_nt(dkv_ref[...], w_ref[:, WQ:])
    back, gain_grad = norm_back(h_ref[...].astype(F32), gain_ref[...], d_normed)
    d_hidden = dm_ref[...] + back
    dh_ref[...] = d_hidden
    low_ref[...] = d_hidden.astype(BF16)
    gain_grad_ref[...] = gain_grad


def d_hidden(dq, dkv, cosine, sine, w_qkv, hidden, gain, d_mid):
    rows, model = hidden.shape
    return kernel(
        d_hidden_kernel,
        2 * rows * w_qkv.size,
        2 * w_qkv.size + 16 * hidden.size,
        out_shape=(
            shape_of(rows, 2 * WK),
            shape_of(rows, model, F32),
            shape_of(rows, model),
            shape_of(1, model, F32),
        ),
    )(dq, *dkv, cosine, sine, w_qkv, hidden, gain, d_mid)


def forward_layer(hidden, weights, place, tick):
    w_qkv, w_out, w_gate, w_up, w_down, gain_attn, gain_ffn = weights
    group, cosine, sine, bias = place
    normed, queries, kv_own = project(hidden, gain_attn, w_qkv, cosine, sine)
    kv_all = jnp.concatenate(flip_gather(kv_own, group), axis=0)
    mixed, lse = attend_forward(queries, kv_all, bias)
    middle, ffn_in = mix(mixed, w_out, hidden, gain_ffn)
    inner, *slopes = gate_up(ffn_in, w_gate, w_up, tick != "a")
    out, low = down(inner, w_down, middle)
    return out, low, (hidden, normed, queries, kv_all, lse, mixed, middle, ffn_in, inner, slopes)


def backward_layer(grad, kept, weights, place):
    w_qkv, w_out, w_gate, w_up, w_down, gain_attn, gain_ffn = weights
    group, cosine, sine, bias = place
    hidden, normed, queries, kv_all, lse, mixed, middle, ffn_in, inner, slopes = kept
    d_gu = d_inner(grad, w_down, *slopes)
    d_mid, mid_low, d_mixed, gain_ffn_grad = d_middle(
        d_gu, w_gate, w_up, middle, gain_ffn, grad, w_out
    )
    d_q, *d_kv = attend_backward(queries, kv_all, d_mixed, bias, lse, cosine, sine)
    dk, dk2 = flip_reduce(d_kv[0::2], group)
    dv, dv2 = flip_reduce(d_kv[1::2], group)
    d_kv, d_hid, hid_low, gain_attn_grad = d_hidden(
        d_q, (dk, dv, dk2, dv2), cosine, sine, w_qkv, hidden, gain_attn, d_mid
    )
    pairs = {
        "d": (inner, (grad,)),
        "g": (ffn_in, (d_gu,)),
        "o": (mixed, (mid_low,)),
        "q": (normed, (d_q, d_kv)),
    }
    return d_hid, hid_low, pairs, (gain_attn_grad, gain_ffn_grad)


def grad_kernel(*refs):
    total = (len(refs) - 2) // 3
    for lefts, out in ((refs[:total], refs[-2]), (refs[total : 2 * total], refs[-1])):
        product = None
        for left, right in zip(lefts, refs[2 * total : 3 * total]):
            operand = right[0] if len(right.shape) == 3 else right[...]
            term = dot_nn(left[...], operand)
            product = term if product is None else product + term
        out[...] = product.astype(BF16)


def grad_product(lefts, rights, depth, row, rows, plane, col, cols, tile_cols):
    tokens = rights[0].shape[-2]
    first_col = col // tile_cols
    left = lambda base: pl.BlockSpec((rows, tokens), lambda j: (base, 0))
    if rights[0].ndim == 3:
        right = pl.BlockSpec((1, tokens, tile_cols), lambda j: (plane, 0, first_col + j))
    else:
        right = pl.BlockSpec((tokens, tile_cols), lambda j: (0, first_col + j))
    out = pl.BlockSpec((rows, tile_cols), lambda j: (0, j))
    total = len(lefts)
    return kernel(
        grad_kernel,
        4 * total * tokens * rows * cols,
        8 * rows * cols,
        grid=(cols // tile_cols,),
        in_specs=[left((depth + row) // rows)] * total + [left(row // rows)] * total + [right] * total,
        out_specs=[out, out],
        out_shape=(shape_of(rows, cols), shape_of(rows, cols)),
    )(*lefts, *lefts, *rights)


def left_rows(left, me, count, group):
    left_t = left.T
    depth = left_t.shape[0] // count

    def rows_of(p):
        first = lax.dynamic_slice_in_dim(left_t, (me ^ p) * depth, depth, 0)
        second = lax.dynamic_slice_in_dim(left_t, (me ^ p ^ group) * depth, depth, 0)
        return jnp.concatenate([first, second], axis=0)

    return [rows_of(0)] + [flip(rows_of(p), p) for p in range(1, group)]


def right_rows(right, group):
    return [right] + [flip(right, p) for p in range(1, group)]


def reduced(other, own, group):
    return rep_sum(own + flip(other, group))


def shards(
    inputs,
    w_query,
    w_key,
    w_value,
    w_out,
    w_gate,
    w_up,
    w_down,
    norm_attn,
    norm_ffn,
    image_start,
    cotangent,
):
    is_first = lax.axis_index("section") == 0
    me = lax.axis_index("seq")
    count = lax.axis_size("seq")
    micro_count, _, piece_rows, half_width = inputs.shape
    group = count // micro_count
    micro = me // group
    own_input = inputs[:, 0]
    own_cotan = cotangent[:, 0]
    incoming = flip(jnp.where(is_first, own_cotan, own_input), 1, "section")
    whole = jnp.where(
        is_first,
        jnp.concatenate([own_input, incoming], axis=-1),
        jnp.concatenate([incoming, own_cotan], axis=-1),
    )
    kept_block = lax.dynamic_index_in_dim(whole, micro, 0, keepdims=False)
    sent_block = lax.dynamic_index_in_dim(whole, 1 - micro, 0, keepdims=False)
    given = jnp.concatenate([kept_block, flip(sent_block, group)], axis=0)

    def positions(device):
        within = jnp.arange(piece_rows, dtype=jnp.int32)
        return jnp.concatenate(
            [device * piece_rows + within, (device ^ group) * piece_rows + within]
        )

    query_pos = positions(me)
    key_pos = jnp.concatenate([positions(me ^ p) for p in range(group)])
    start = lax.dynamic_index_in_dim(image_start[:, 0], micro, 0, keepdims=False)
    query_in = (query_pos >= start) & (query_pos < start + IMG)
    key_in = (key_pos >= start) & (key_pos < start + IMG)
    allowed = (key_pos[:, None] <= query_pos[None, :]) | (key_in[:, None] & query_in[None, :])
    bias = jnp.where(allowed, 0.0, masked_value).astype(F32)
    frequency = 10000.0 ** (-jnp.arange(DH // 2, dtype=F32) / (DH // 2))
    angles = query_pos.astype(F32)[:, None] * frequency[None, :]
    cosine = jnp.tile(jnp.cos(angles), (1, 4))
    sine = jnp.sin(angles)
    sine = jnp.concatenate([-sine, sine, -sine, sine], axis=1)
    place = (group, cosine, sine, bias)

    gains = flip_gather(jnp.stack([norm_attn[0], norm_ffn[0]]), count)
    gains = put_rows(gains, [me ^ p for p in range(count)]).reshape(count, 2, -1)
    gains = gains.transpose(1, 0, 2).reshape(2, 1, -1).astype(F32)
    qkv_shard = jnp.concatenate([w_query[0], w_key[0], w_value[0]], axis=1)
    weights = (
        gather_rows(qkv_shard, count, me),
        gather_rows(w_out[0], count, me),
        gather_over_rep(w_gate[0], count, me),
        gather_over_rep(w_up[0], count, me),
        gather_rows(w_down[0], count, me),
        gains[0],
        gains[1],
    )

    _, low, _ = forward_layer(given, weights, place, "a")
    received = shifted(low, "section", 1)
    layer_in = jnp.where(is_first, given, received)
    block, _, kept = forward_layer(layer_in, weights, place, "b")
    _, low, _, _ = backward_layer(given, kept, weights, place)
    received = shifted(low, "section", -1)
    out_grad = jnp.where(is_first, received, given)
    first_grad, _, pairs, gain_grads = backward_layer(out_grad, kept, weights, place)

    lefts = {k: left_rows(v[0], me, count, group) for k, v in pairs.items()}
    rights = {k: [right_rows(right, group) for right in v[1]] for k, v in pairs.items()}
    depths = {k: v[0].shape[1] // count for k, v in pairs.items()}
    gain_sums = jnp.concatenate(gain_grads, axis=0)
    for bit in bits_below(group):
        gain_sums = gain_sums + flip(gain_sums, bit)
    gain_sums = gain_sums.reshape(2, count, depths["q"]).transpose(1, 2, 0).astype(BF16)

    def chunk(name, part, row, rows, plane, col, cols, tile_cols, gained=False):
        k = name[0]
        other, own = grad_product(
            lefts[k], rights[k][part], depths[k], row, rows, plane, col, cols, tile_cols
        )
        if gained:
            other, own = with_gains(other, me ^ group), with_gains(own, me)
        return reduced(other, own, group)

    def with_gains(product, device):
        extra = lax.dynamic_index_in_dim(gain_sums, device, 0, keepdims=False)
        return jnp.concatenate([product, jnp.pad(extra, ((0, 0), (0, KT - 2)))], axis=1)

    model = half_width * 2
    half, depth = depths["d"] // 2, depths["g"]
    wide = w_gate.shape[2] // 2
    d_grad = [chunk(f"d{i}", 0, i * half, half, 0, 0, model, model // 3) for i in range(2)]
    gu_grad = [
        chunk(f"g{i}", 0, 0, depth, i // 2, (i % 2) * wide, wide, wide // 3) for i in range(4)
    ]
    o_grad = chunk("o", 0, 0, depths["o"], 0, 0, model, WK)
    q_grad = chunk("q", 0, 0, depths["q"], 0, 0, WQ, WK)
    kv_grad = chunk("qkv", 1, 0, depths["q"], 0, 0, 2 * WK, WK, True)

    def placed(result, from_first):
        kept_rows, sent_rows = result[:piece_rows], result[piece_rows:]
        back = flip(sent_rows.astype(BF16), group).astype(F32)
        first = jnp.where(micro == 0, kept_rows, back)
        second = jnp.where(micro == 0, back, kept_rows)
        rows = jnp.stack([first, second])
        low, high = rows[..., :half_width], rows[..., half_width:]
        if from_first:
            arrived = shifted(high.astype(BF16), "section", 1)
            return jnp.where(is_first, low, arrived.astype(F32))
        arrived = shifted(low.astype(BF16), "section", -1)
        return jnp.where(is_first, arrived.astype(F32), high)

    block_out = placed(block, False)[:, None]
    input_grad = placed(first_grad, True)[:, None]
    grads = [
        q_grad,
        kv_grad[:, :WK],
        kv_grad[:, WK : 2 * WK],
        o_grad,
        jnp.concatenate(gu_grad[:2], axis=1),
        jnp.concatenate(gu_grad[2:], axis=1),
        jnp.concatenate(d_grad, axis=0),
        kv_grad[:, 2 * WK],
        kv_grad[:, 2 * WK + 1],
    ]
    return (block_out, input_grad) + tuple(grad.astype(F32)[None] for grad in grads)


def solution(mesh):
    rows = P("section", "seq", None)
    tokens = P(None, "rep", "seq", "section")
    in_specs = (tokens,) + (rows,) * 7 + (P("section", "seq"),) * 2 + (P(None, "rep"), tokens)
    out_specs = (tokens, tokens) + (rows,) * 7 + (P("section", "seq"),) * 2

    return jax.shard_map(shards, mesh=mesh, in_specs=in_specs, out_specs=out_specs, check_vma=False)
```

```python
import functools

import jax
import jax.numpy as jnp
from jax import lax
from jax.experimental import pallas as pl
from jax.experimental.pallas import tpu as pltpu
from jax.sharding import PartitionSpec as P

HQ = 18
KVH = 6
DH = 64
IMG = 256
GROUP = HQ // KVH
PAIRS = KVH // 2
QT = 2 * GROUP * DH
KT = 2 * DH
WQ = HQ * DH
WK = KVH * DH
masked_value = -1e30
F32 = jnp.float32
BF16 = jnp.bfloat16


def flip(block, bit, axis="seq"):
    return lax.ppermute(block, axis, [(i, i ^ bit) for i in range(lax.axis_size(axis))])


def shifted(block, axis, distance):
    devices = range(lax.axis_size(axis))
    route = [(i - distance, i) for i in devices if i - distance in devices]
    return lax.ppermute(block, axis, route)


def bits_below(count):
    return [1 << i for i in range(count.bit_length() - 1)]


def flip_gather(block, count):
    held = {0: block}
    for bit in reversed(bits_below(count)):
        held.update({p | bit: flip(piece, bit) for p, piece in list(held.items())})
    return [held[p] for p in range(count)]


def flip_reduce(pieces, count):
    held = dict(enumerate(pieces))
    for bit in bits_below(count):
        kept = [p for p in held if not p & bit]
        last = 2 * bit == count
        added = {p: flip(held[p | bit], bit) for p in kept}
        if last:
            return held[0], added[0]
        held = {p: held[p] + added[p] for p in kept}


def row_pieces(shard, count):
    return {"pieces": flip_gather(shard, count), "parts": None}


def column_pieces(shard, count):
    reps = lax.axis_size("rep")
    if count != 4 or reps != 4:
        return row_pieces(shard, count)
    here = lax.axis_index("rep")
    width = shard.shape[1] // reps
    part = flip(lax.dynamic_slice_in_dim(shard, here * width, width, 1), 2)
    parts = [part] + [
        lax.ppermute(part, "rep", [(i, (i + k) % reps) for i in range(reps)])
        for k in range(1, reps)
    ]
    across = [flip(piece, 1) for piece in parts]
    return {"pieces": [shard, flip(shard, 1)], "parts": (parts, across)}


def arrays_of(weight):
    if weight["parts"] is None:
        return weight["pieces"]
    return weight["pieces"] + weight["parts"][0] + weight["parts"][1]


def copies_of(weight, refs, ids_ref, tile, width, target, sems):
    pieces = len(weight["pieces"])
    depth = weight["pieces"][0].shape[0]
    me = ids_ref[0]
    column = tile_column(weight, ids_ref, tile) * width
    if not isinstance(column, int):
        column = pl.multiple_of(column, width)

    def rows(p):
        return pl.ds(pl.multiple_of((me ^ p) * depth, depth), depth)

    copies = [
        pltpu.make_async_copy(
            refs[p].at[:, pl.ds(column, width)], target.at[rows(p), :], sems.at[p]
        )
        for p in range(pieces)
    ]
    if weight["parts"] is not None:
        total = len(weight["parts"][0])
        for p in (2, 3):
            ref = refs[pieces + (p - 2) * total + tile]
            copies.append(pltpu.make_async_copy(ref, target.at[rows(p), :], sems.at[p]))
    return copies


def tile_column(weight, ids_ref, tile):
    if weight["parts"] is None:
        return tile
    total = len(weight["parts"][0])
    return lax.rem(ids_ref[1] + (total - tile), total)


def when_step(steps, body):
    for step in range(steps):
        pl.when(pl.program_id(0) == step)(functools.partial(body, step))


def rep_sum(value):
    count = lax.axis_size("rep")
    if count != 4:
        return lax.psum(value, "rep").astype(BF16)
    here = lax.axis_index("rep")
    inner = (here == 1) | (here == 2)
    arrived = lax.ppermute(value, "rep", [(0, 1), (3, 2)])
    value = plus(value, arrived)
    arrived = lax.ppermute(value, "rep", [(1, 2), (2, 1)])
    value = plus(value, arrived)
    arrived = lax.ppermute(value, "rep", [(1, 0), (2, 3)])
    return jnp.where(inner, value, arrived)


def plus(left, right):
    def body(left_ref, right_ref, out_ref):
        out_ref[...] = left_ref[...] + right_ref[...]

    rows, cols = left.shape
    return kernel(
        body, left.size, 6 * left.size, vmem=4, out_shape=shape_of(rows, cols)
    )(left, right)


def dot_nn(left, right):
    return jnp.dot(left, right, preferred_element_type=F32)


def dot_nt(left, right):
    return lax.dot_general(left, right, (((1,), (1,)), ((), ())), preferred_element_type=F32)


def inverse_rms(hidden):
    return lax.rsqrt(jnp.mean(hidden * hidden, axis=-1, keepdims=True) + 1e-05)


def kernel(body, flops, size, scalars=0, vmem=12, **options):
    cost = pl.CostEstimate(flops=flops, bytes_accessed=size, transcendentals=0)
    if scalars:
        fields = ("grid", "in_specs", "out_specs", "scratch_shapes")
        options["grid_spec"] = pltpu.PrefetchScalarGridSpec(
            num_scalar_prefetch=scalars, **{k: options.pop(k) for k in fields if k in options}
        )
    params = pltpu.CompilerParams(vmem_limit_bytes=vmem << 20)
    return pl.pallas_call(body, cost_estimate=cost, compiler_params=params, **options)


def shape_of(rows, cols, kind=BF16):
    return jax.ShapeDtypeStruct((rows, cols), kind)


ANY = pl.BlockSpec(memory_space=pl.ANY)


def fixed(*extent):
    return pl.BlockSpec(extent, lambda *step: (0,) * len(extent))


def other_half(tile):
    lane = lax.broadcasted_iota(jnp.int32, tile.shape, 1)
    low = lane % DH < DH // 2
    return jnp.where(low, pltpu.roll(tile, KT - DH // 2, 1), pltpu.roll(tile, DH // 2, 1))


def project(ids, hidden, gain, w_qkv, cosine, sine):
    rows, model = hidden.shape
    arrays = arrays_of(w_qkv)
    steps = GROUP + 2

    def body(ids_ref, h_ref, gain_ref, cos_ref, sin_ref, *rest):
        w_refs, (normed_ref, q_ref, kv_ref, buffer, sems) = rest[: len(arrays)], rest[len(arrays) :]
        step = pl.program_id(0)
        batches = [
            copies_of(w_qkv, w_refs, ids_ref, k, WK, buffer.at[k], sems.at[k]) for k in range(steps)
        ]

        @pl.when(step == 0)
        def _():
            for batch in batches:
                for copy in batch:
                    copy.start()
            hidden = h_ref[...].astype(F32)
            normed_ref[...] = (hidden * inverse_rms(hidden) * gain_ref[...]).astype(BF16)

        def wait(k):
            for copy in batches[k]:
                copy.wait()

        when_step(steps, wait)
        product = dot_nn(normed_ref[...], buffer[step])

        def turned(scale, out_ref):
            for start in range(0, WK, KT):
                tile = product[:, start : start + KT]
                result = tile * cos_ref[...] + other_half(tile) * sin_ref[...]
                out_ref[:, start : start + KT] = (result * scale).astype(BF16)

        @pl.when(step < GROUP)
        def _():
            turned(DH ** (-0.5), q_ref)

        @pl.when(step == GROUP)
        def _():
            turned(1.0, kv_ref)

        @pl.when(step == GROUP + 1)
        def _():
            kv_ref[...] = product.astype(BF16)

    return kernel(
        body,
        2 * rows * model * steps * WK,
        2 * model * steps * WK + 8 * hidden.size,
        scalars=1,
        grid=(steps,),
        in_specs=[fixed(rows, model), fixed(1, model), fixed(rows, KT), fixed(rows, KT)]
        + [ANY] * len(arrays),
        out_specs=[
            fixed(rows, model),
            pl.BlockSpec((rows, WK), lambda j, ids: (0, jnp.minimum(j, GROUP - 1))),
            pl.BlockSpec((rows, WK), lambda j, ids: (0, jnp.maximum(j - GROUP, 0))),
        ],
        out_shape=(shape_of(rows, model), shape_of(rows, WQ), shape_of(rows, 2 * WK)),
        scratch_shapes=[
            pltpu.VMEM((steps, model, WK), BF16),
            pltpu.SemaphoreType.DMA((steps, len(arrays))),
        ],
    )(ids, hidden, gain, cosine, sine, *arrays)


def attend_kernel(q_ref, k_ref, v_ref, bias_ref, o_ref, lse_ref):
    bias = bias_ref[...]
    values_t = v_ref[...].T
    for tile in range(GROUP):
        queries_t = q_ref[:, tile * KT : (tile + 1) * KT].T
        outs = []
        for half in range(2):
            head = 2 * tile + half
            kv = head // GROUP
            keys = k_ref[:, kv * DH : (kv + 1) * DH]
            logits = dot_nn(keys, queries_t[half * DH : (half + 1) * DH]) + bias
            top = jnp.max(logits, axis=0, keepdims=True)
            exponent = jnp.exp(logits - top)
            total = jnp.sum(exponent, axis=0, keepdims=True)
            attend = (exponent * (1.0 / total)).astype(BF16)
            outs.append(dot_nn(values_t[kv * DH : (kv + 1) * DH], attend))
            lse_ref[0, head : head + 1, :] = top + jnp.log(total)
        joined = jnp.concatenate(outs, axis=0).T
        o_ref[:, tile * KT : (tile + 1) * KT] = joined.astype(BF16)


def attend_forward(queries, keys_values, bias):
    rows, length = queries.shape[0], keys_values.shape[0]
    count = HQ * rows * length
    return kernel(
        attend_kernel,
        count * 8 * DH,
        4 << 20,
        grid=(PAIRS,),
        in_specs=[
            pl.BlockSpec((rows, QT), lambda i: (0, i)),
            pl.BlockSpec((length, KT), lambda i: (0, i)),
            pl.BlockSpec((length, KT), lambda i: (0, i + PAIRS)),
            fixed(length, rows),
        ],
        out_specs=[
            pl.BlockSpec((rows, QT), lambda i: (0, i)),
            pl.BlockSpec((1, 8, rows), lambda i: (i, 0, 0)),
        ],
        out_shape=(shape_of(rows, WQ), jax.ShapeDtypeStruct((PAIRS, 8, rows), F32)),
    )(queries, keys_values, keys_values, bias)


def attend_back_kernel(
    q_ref, k_ref, v_ref, do_ref, bias_ref, lse_ref, cos_ref, sin_ref, dq_ref, *dkv_refs
):
    bias = bias_ref[...]
    keys_t = k_ref[...].T
    dk = [None, None]
    dv = [None, None]
    for tile in range(GROUP):
        q_tile = q_ref[:, tile * KT : (tile + 1) * KT]
        do_tile = do_ref[:, tile * KT : (tile + 1) * KT]
        queries_t = q_tile.T
        do_t = do_tile.T
        grads = []
        for half in range(2):
            head = 2 * tile + half
            kv = head // GROUP
            span = slice(half * DH, (half + 1) * DH)
            kv_span = slice(kv * DH, (kv + 1) * DH)
            logits = dot_nn(k_ref[:, kv_span], queries_t[span]) + bias
            attend = jnp.exp(logits - lse_ref[0, head : head + 1, :])
            d_attend = dot_nn(v_ref[:, kv_span], do_t[span])
            delta = jnp.sum(d_attend * attend, axis=0, keepdims=True)
            d_scores = (attend * (d_attend - delta)).astype(BF16)
            grads.append(dot_nn(keys_t[kv_span], d_scores))
            dk_term = dot_nn(d_scores, q_tile[:, span])
            dv_term = dot_nn(attend.astype(BF16), do_tile[:, span])
            dk[kv] = dk_term if dk[kv] is None else dk[kv] + dk_term
            dv[kv] = dv_term if dv[kv] is None else dv[kv] + dv_term
        joined = jnp.concatenate(grads, axis=0).T * DH ** (-0.5)
        turned = joined * cos_ref[...] - other_half(joined) * sin_ref[...]
        dq_ref[:, tile * KT : (tile + 1) * KT] = turned.astype(BF16)
    d_keys = jnp.concatenate(dk, axis=1).astype(BF16)
    d_values = jnp.concatenate(dv, axis=1).astype(BF16)
    rows = dq_ref.shape[0]
    for p in range(len(dkv_refs) // 2):
        dkv_refs[2 * p][...] = d_keys[p * rows : (p + 1) * rows]
        dkv_refs[2 * p + 1][...] = d_values[p * rows : (p + 1) * rows]


def attend_backward(queries, keys_values, d_mixed, bias, lse, cosine, sine):
    rows, length = queries.shape[0], keys_values.shape[0]
    count = HQ * rows * length
    narrow = pl.BlockSpec((rows, KT), lambda i: (0, i))
    total = 2 * (length // rows)
    return kernel(
        attend_back_kernel,
        count * 16 * DH,
        8 << 20,
        grid=(PAIRS,),
        in_specs=[
            pl.BlockSpec((rows, QT), lambda i: (0, i)),
            pl.BlockSpec((length, KT), lambda i: (0, i)),
            pl.BlockSpec((length, KT), lambda i: (0, i + PAIRS)),
            pl.BlockSpec((rows, QT), lambda i: (0, i)),
            fixed(length, rows),
            pl.BlockSpec((1, 8, rows), lambda i: (i, 0, 0)),
            fixed(rows, KT),
            fixed(rows, KT),
        ],
        out_specs=[pl.BlockSpec((rows, QT), lambda i: (0, i))] + [narrow] * total,
        out_shape=(shape_of(rows, WQ),) + (shape_of(rows, WK),) * total,
    )(queries, keys_values, keys_values, d_mixed, bias, lse, cosine, sine)


def mix(ids, mixed, w_out, hidden, gain):
    rows, model = hidden.shape
    arrays = arrays_of(w_out)
    steps = model // WK

    def body(ids_ref, mixed_ref, h_ref, gain_ref, *rest):
        w_refs, (middle_ref, ffn_ref, buffer, sems) = rest[: len(arrays)], rest[len(arrays) :]
        batches = [
            copies_of(w_out, w_refs, ids_ref, k, WK, buffer.at[k], sems.at[k]) for k in range(steps)
        ]
        for batch in batches:
            for copy in batch:
                copy.start()
        for k in range(steps):
            for copy in batches[k]:
                copy.wait()
            span = slice(k * WK, (k + 1) * WK)
            product = dot_nn(mixed_ref[...], buffer[k])
            middle_ref[:, span] = h_ref[:, span].astype(F32) + product
        middle = middle_ref[...]
        ffn_ref[...] = (middle * inverse_rms(middle) * gain_ref[...]).astype(BF16)

    return kernel(
        body,
        2 * rows * WQ * model,
        2 * WQ * model + 8 * hidden.size,
        scalars=1,
        grid=(1,),
        in_specs=[fixed(rows, WQ), fixed(rows, model), fixed(1, model)] + [ANY] * len(arrays),
        out_specs=[fixed(rows, model), fixed(rows, model)],
        out_shape=(shape_of(rows, model, F32), shape_of(rows, model)),
        scratch_shapes=[
            pltpu.VMEM((steps, WQ, WK), BF16),
            pltpu.SemaphoreType.DMA((steps, len(arrays))),
        ],
    )(ids, mixed, hidden, gain, *arrays)


FF_TILES = 4


def gate_up(ids, ffn_in, w_gate, w_up, slopes):
    rows, model = ffn_in.shape
    width = w_gate["pieces"][0].shape[1]
    tile = width // FF_TILES
    arrays = arrays_of(w_gate)
    total = len(arrays)
    outs = 3 if slopes else 1

    def body(ids_ref, x_ref, *rest):
        refs = (rest[:total], rest[total : 2 * total])
        out_refs = rest[2 * total : 2 * total + outs]
        buffer, sems = rest[2 * total + outs :]
        step = pl.program_id(0)
        batches = [
            [
                copy
                for i, weight in enumerate((w_gate, w_up))
                for copy in copies_of(
                    weight, refs[i], ids_ref, k, tile, buffer.at[k, i], sems.at[k, i]
                )
            ]
            for k in range(FF_TILES)
        ]

        @pl.when(step == 0)
        def _():
            for batch in batches:
                for copy in batch:
                    copy.start()

        def wait(k):
            for copy in batches[k]:
                copy.wait()

        when_step(FF_TILES, wait)
        gate = dot_nn(x_ref[...], buffer[step, 0])
        up = dot_nn(x_ref[...], buffer[step, 1])
        sig = 1.0 / (1.0 + jnp.exp(-gate))
        silu = gate * sig
        out_refs[0][...] = (silu * up).astype(BF16)
        if slopes:
            out_refs[1][...] = (up * (sig * (1.0 + gate * (1.0 - sig)))).astype(BF16)
            out_refs[2][...] = silu.astype(BF16)

    cols = pl.BlockSpec((rows, tile), lambda j, ids: (0, tile_column(w_gate, ids, j)))
    return kernel(
        body,
        4 * rows * model * width,
        4 * model * width + 2 * outs * rows * width,
        scalars=1,
        vmem=24,
        grid=(FF_TILES,),
        in_specs=[fixed(rows, model)] + [ANY] * (2 * total),
        out_specs=[cols] * outs,
        out_shape=(shape_of(rows, width),) * outs,
        scratch_shapes=[
            pltpu.VMEM((FF_TILES, 2, model, tile), BF16),
            pltpu.SemaphoreType.DMA((FF_TILES, 2, total)),
        ],
    )(ids, ffn_in, *arrays, *arrays_of(w_up))


def piece_block(rows, depth):
    return pl.BlockSpec((rows, depth), lambda j, ids: (0, ids[0] ^ j))


def down(ids, inner, w_down, middle):
    rows, model = middle.shape
    pieces = w_down["pieces"]
    total, depth = len(pieces), pieces[0].shape[0]

    def body(ids_ref, inner_ref, middle_ref, *rest):
        w_refs, (out_ref, low_ref, buffer, sems) = rest[:total], rest[total:]
        step = pl.program_id(0)
        copies = [pltpu.make_async_copy(w_refs[k], buffer.at[k], sems.at[k]) for k in range(total)]

        @pl.when(step == 0)
        def _():
            for copy in copies:
                copy.start()
            out_ref[...] = middle_ref[...]

        when_step(total, lambda k: copies[k].wait())
        out_ref[...] += dot_nn(inner_ref[...], buffer[step])

        @pl.when(step == total - 1)
        def _():
            low_ref[...] = out_ref[...].astype(BF16)

    return kernel(
        body,
        2 * rows * model * depth * total,
        2 * model * depth * total + 12 * middle.size,
        scalars=1,
        vmem=20,
        grid=(total,),
        in_specs=[piece_block(rows, depth), fixed(rows, model)] + [ANY] * total,
        out_specs=[fixed(rows, model), fixed(rows, model)],
        out_shape=(shape_of(rows, model, F32), shape_of(rows, model)),
        scratch_shapes=[
            pltpu.VMEM((total, depth, model), BF16),
            pltpu.SemaphoreType.DMA((total,)),
        ],
    )(ids, inner, middle, *pieces)


def d_inner(ids, grad, w_down, gate_slope, up_slope):
    rows, model = grad.shape
    pieces = w_down["pieces"]
    total, depth = len(pieces), pieces[0].shape[0]

    def body(ids_ref, g_ref, gate_slope_ref, up_slope_ref, *rest):
        w_refs, (out_ref, buffer, sems) = rest[:total], rest[total:]
        step = pl.program_id(0)
        copies = [pltpu.make_async_copy(w_refs[k], buffer.at[k], sems.at[k]) for k in range(total)]

        @pl.when(step == 0)
        def _():
            for copy in copies:
                copy.start()

        when_step(total, lambda k: copies[k].wait())
        product = dot_nt(g_ref[...], buffer[step])
        out_ref[0] = (product * gate_slope_ref[...].astype(F32)).astype(BF16)
        out_ref[1] = (product * up_slope_ref[...].astype(F32)).astype(BF16)

    return kernel(
        body,
        2 * rows * model * depth * total,
        2 * model * depth * total + 8 * rows * depth * total,
        scalars=1,
        vmem=20,
        grid=(total,),
        in_specs=[fixed(rows, model), piece_block(rows, depth), piece_block(rows, depth)]
        + [ANY] * total,
        out_specs=pl.BlockSpec((2, rows, depth), lambda j, ids: (0, 0, ids[0] ^ j)),
        out_shape=jax.ShapeDtypeStruct((2, rows, depth * total), BF16),
        scratch_shapes=[
            pltpu.VMEM((total, depth, model), BF16),
            pltpu.SemaphoreType.DMA((total,)),
        ],
    )(ids, grad, gate_slope, up_slope, *pieces)


def norm_back(hidden, gain, d_normed):
    inverse = inverse_rms(hidden)
    scaled = d_normed * gain
    mean = jnp.mean(scaled * hidden, axis=-1, keepdims=True)
    back = inverse * (scaled - hidden * (inverse * inverse) * mean)
    return back, jnp.sum(d_normed * hidden * inverse, axis=0, keepdims=True)


def d_middle(ids, d_gu, w_gate, w_up, middle, gain, grad, w_out):
    rows, model = middle.shape
    width = w_gate["pieces"][0].shape[1]
    tile = width // FF_TILES
    arrays, out_arrays = arrays_of(w_gate), arrays_of(w_out)
    total, out_total = len(arrays), len(out_arrays)

    def body(ids_ref, d_ref, middle_ref, gain_ref, g_ref, *rest):
        refs = (rest[:total], rest[total : 2 * total])
        out_refs = rest[2 * total : 2 * total + out_total]
        dm_ref, low_ref, mixed_ref, gain_grad_ref, sum_ref, buffer, sems, last, last_sems = rest[
            2 * total + out_total :
        ]
        step = pl.program_id(0)
        batches = [
            [
                copy
                for i, weight in enumerate((w_gate, w_up))
                for copy in copies_of(
                    weight, refs[i], ids_ref, k, tile, buffer.at[k, i], sems.at[k, i]
                )
            ]
            for k in range(FF_TILES)
        ]
        last_copies = copies_of(w_out, out_refs, ids_ref, 0, model, last, last_sems)

        @pl.when(step == 0)
        def _():
            for batch in batches + [last_copies]:
                for copy in batch:
                    copy.start()

        def wait(k):
            for copy in batches[k]:
                copy.wait()

        when_step(FF_TILES, wait)
        term = dot_nt(d_ref[0], buffer[step, 0]) + dot_nt(d_ref[1], buffer[step, 1])

        @pl.when(step == 0)
        def _():
            sum_ref[...] = term

        @pl.when(step > 0)
        def _():
            sum_ref[...] += term

        @pl.when(step == FF_TILES - 1)
        def _():
            back, gain_grad = norm_back(middle_ref[...], gain_ref[...], sum_ref[...])
            d_middle = g_ref[...].astype(F32) + back
            dm_ref[...] = d_middle
            low_ref[...] = d_middle.astype(BF16)
            gain_grad_ref[...] = gain_grad
            for copy in last_copies:
                copy.wait()
            mixed_ref[...] = dot_nt(low_ref[...], last[...]).astype(BF16)

    columns = pl.BlockSpec((2, rows, tile), lambda j, ids: (0, 0, tile_column(w_gate, ids, j)))
    return kernel(
        body,
        4 * rows * model * width + 2 * rows * model * WQ,
        4 * model * width + 4 * rows * width + 12 * middle.size,
        scalars=1,
        vmem=32,
        grid=(FF_TILES,),
        in_specs=[columns, fixed(rows, model), fixed(1, model), fixed(rows, model)]
        + [ANY] * (2 * total + out_total),
        out_specs=[fixed(rows, model)] * 2 + [fixed(rows, WQ), fixed(1, model)],
        out_shape=(
            shape_of(rows, model, F32),
            shape_of(rows, model),
            shape_of(rows, WQ),
            shape_of(1, model, F32),
        ),
        scratch_shapes=[
            pltpu.VMEM((rows, model), F32),
            pltpu.VMEM((FF_TILES, 2, model, tile), BF16),
            pltpu.SemaphoreType.DMA((FF_TILES, 2, total)),
            pltpu.VMEM((WQ, model), BF16),
            pltpu.SemaphoreType.DMA((out_total,)),
        ],
    )(ids, d_gu, middle, gain, grad, *arrays, *arrays_of(w_up), *out_arrays)


def d_hidden(ids, dq, dkv, cosine, sine, w_qkv, hidden, gain, d_mid):
    rows, model = hidden.shape
    arrays = arrays_of(w_qkv)
    steps = GROUP + 2

    def body(
        ids_ref, dq_ref, dk_ref, dv_ref, dk2_ref, dv2_ref, cos_ref, sin_ref, h_ref, gain_ref,
        dm_ref, *rest,
    ):
        w_refs = rest[: len(arrays)]
        dkv_ref, dh_ref, low_ref, gain_grad_ref, buffer, sems = rest[len(arrays) :]
        batches = [
            copies_of(w_qkv, w_refs, ids_ref, k, WK, buffer.at[k], sems.at[k]) for k in range(steps)
        ]
        for batch in batches:
            for copy in batch:
                copy.start()
        for start in range(0, WK, KT):
            tile = dk_ref[:, start : start + KT].astype(F32)
            tile += dk2_ref[:, start : start + KT].astype(F32)
            turned = tile * cos_ref[...] - other_half(tile) * sin_ref[...]
            dkv_ref[:, start : start + KT] = turned.astype(BF16)
        dkv_ref[:, WK:] = (dv_ref[...].astype(F32) + dv2_ref[...].astype(F32)).astype(BF16)
        d_normed = None
        for k in range(steps):
            for copy in batches[k]:
                copy.wait()
            if k < GROUP:
                operand = dq_ref[:, k * WK : (k + 1) * WK]
            else:
                operand = dkv_ref[:, (k - GROUP) * WK : (k - GROUP + 1) * WK]
            term = dot_nt(operand, buffer[k])
            d_normed = term if d_normed is None else d_normed + term
        back, gain_grad = norm_back(h_ref[...].astype(F32), gain_ref[...], d_normed)
        d_hidden = dm_ref[...] + back
        dh_ref[...] = d_hidden
        low_ref[...] = d_hidden.astype(BF16)
        gain_grad_ref[...] = gain_grad

    narrow = fixed(rows, WK)
    return kernel(
        body,
        2 * rows * model * steps * WK,
        2 * model * steps * WK + 16 * hidden.size,
        scalars=1,
        grid=(1,),
        in_specs=[fixed(rows, WQ)]
        + [narrow] * 4
        + [fixed(rows, KT)] * 2
        + [fixed(rows, model), fixed(1, model), fixed(rows, model)]
        + [ANY] * len(arrays),
        out_specs=[fixed(rows, 2 * WK), fixed(rows, model), fixed(rows, model), fixed(1, model)],
        out_shape=(
            shape_of(rows, 2 * WK),
            shape_of(rows, model, F32),
            shape_of(rows, model),
            shape_of(1, model, F32),
        ),
        scratch_shapes=[
            pltpu.VMEM((steps, model, WK), BF16),
            pltpu.SemaphoreType.DMA((steps, len(arrays))),
        ],
    )(ids, dq, *dkv, cosine, sine, hidden, gain, d_mid, *arrays)


def forward_layer(hidden, weights, place, tick):
    w_qkv, w_out, w_gate, w_up, w_down, gain_attn, gain_ffn = weights
    ids, group, cosine, sine, bias = place
    normed, queries, kv_own = project(ids, hidden, gain_attn, w_qkv, cosine, sine)
    kv_all = jnp.concatenate(flip_gather(kv_own, group), axis=0)
    mixed, lse = attend_forward(queries, kv_all, bias)
    middle, ffn_in = mix(ids, mixed, w_out, hidden, gain_ffn)
    inner, *slopes = gate_up(ids, ffn_in, w_gate, w_up, tick != "a")
    out, low = down(ids, inner, w_down, middle)
    return out, low, (hidden, normed, queries, kv_all, lse, mixed, middle, ffn_in, inner, slopes)


def backward_layer(grad, kept, weights, place):
    w_qkv, w_out, w_gate, w_up, w_down, gain_attn, gain_ffn = weights
    ids, group, cosine, sine, bias = place
    hidden, normed, queries, kv_all, lse, mixed, middle, ffn_in, inner, slopes = kept
    d_gu = d_inner(ids, grad, w_down, *slopes)
    d_mid, mid_low, d_mixed, gain_ffn_grad = d_middle(
        ids, d_gu, w_gate, w_up, middle, gain_ffn, grad, w_out
    )
    d_q, *d_kv = attend_backward(queries, kv_all, d_mixed, bias, lse, cosine, sine)
    dk, dk2 = flip_reduce(d_kv[0::2], group)
    dv, dv2 = flip_reduce(d_kv[1::2], group)
    d_kv, d_hid, hid_low, gain_attn_grad = d_hidden(
        ids, d_q, (dk, dv, dk2, dv2), cosine, sine, w_qkv, hidden, gain_attn, d_mid
    )
    pairs = {
        "d": (inner, (grad,)),
        "g": (ffn_in, (d_gu,)),
        "o": (mixed, (mid_low,)),
        "q": (normed, (d_q, d_kv)),
    }
    return d_hid, hid_low, pairs, (gain_attn_grad, gain_ffn_grad)


def grad_kernel(*refs):
    total = (len(refs) - 2) // 3
    for lefts, out in ((refs[:total], refs[-2]), (refs[total : 2 * total], refs[-1])):
        product = None
        for left, right in zip(lefts, refs[2 * total : 3 * total]):
            operand = right[0] if len(right.shape) == 3 else right[...]
            term = dot_nn(left[...], operand)
            product = term if product is None else product + term
        out[...] = product.astype(BF16)


def grad_product(lefts, rights, depth, row, rows, plane, col, cols, tile_cols):
    tokens = rights[0].shape[-2]
    first_col = col // tile_cols
    left = lambda base: pl.BlockSpec((rows, tokens), lambda j: (base, 0))
    if rights[0].ndim == 3:
        right = pl.BlockSpec((1, tokens, tile_cols), lambda j: (plane, 0, first_col + j))
    else:
        right = pl.BlockSpec((tokens, tile_cols), lambda j: (0, first_col + j))
    out = pl.BlockSpec((rows, tile_cols), lambda j: (0, j))
    total = len(lefts)
    return kernel(
        grad_kernel,
        4 * total * tokens * rows * cols,
        8 * rows * cols,
        grid=(cols // tile_cols,),
        in_specs=[left((depth + row) // rows)] * total + [left(row // rows)] * total + [right] * total,
        out_specs=[out, out],
        out_shape=(shape_of(rows, cols), shape_of(rows, cols)),
    )(*lefts, *lefts, *rights)


def left_rows(left, me, count, group):
    left_t = left.T
    depth = left_t.shape[0] // count

    def rows_of(p):
        first = lax.dynamic_slice_in_dim(left_t, (me ^ p) * depth, depth, 0)
        second = lax.dynamic_slice_in_dim(left_t, (me ^ p ^ group) * depth, depth, 0)
        return jnp.concatenate([first, second], axis=0)

    return [rows_of(0)] + [flip(rows_of(p), p) for p in range(1, group)]


def right_rows(right, group):
    return [right] + [flip(right, p) for p in range(1, group)]


def reduced(other, own, group):
    return rep_sum(plus(own, flip(other, group)))


def shards(
    inputs,
    w_query,
    w_key,
    w_value,
    w_out,
    w_gate,
    w_up,
    w_down,
    norm_attn,
    norm_ffn,
    image_start,
    cotangent,
):
    is_first = lax.axis_index("section") == 0
    me = lax.axis_index("seq")
    count = lax.axis_size("seq")
    micro_count, _, piece_rows, half_width = inputs.shape
    group = count // micro_count
    micro = me // group
    own_input = inputs[:, 0]
    own_cotan = cotangent[:, 0]
    incoming = flip(jnp.where(is_first, own_cotan, own_input), 1, "section")
    whole = jnp.where(
        is_first,
        jnp.concatenate([own_input, incoming], axis=-1),
        jnp.concatenate([incoming, own_cotan], axis=-1),
    )
    kept_block = lax.dynamic_index_in_dim(whole, micro, 0, keepdims=False)
    sent_block = lax.dynamic_index_in_dim(whole, 1 - micro, 0, keepdims=False)
    given = jnp.concatenate([kept_block, flip(sent_block, group)], axis=0)

    def positions(device):
        within = jnp.arange(piece_rows, dtype=jnp.int32)
        return jnp.concatenate(
            [device * piece_rows + within, (device ^ group) * piece_rows + within]
        )

    query_pos = positions(me)
    key_pos = jnp.concatenate([positions(me ^ p) for p in range(group)])
    start = lax.dynamic_index_in_dim(image_start[:, 0], micro, 0, keepdims=False)
    query_in = (query_pos >= start) & (query_pos < start + IMG)
    key_in = (key_pos >= start) & (key_pos < start + IMG)
    allowed = (key_pos[:, None] <= query_pos[None, :]) | (key_in[:, None] & query_in[None, :])
    bias = jnp.where(allowed, 0.0, masked_value).astype(F32)
    frequency = 10000.0 ** (-jnp.arange(DH // 2, dtype=F32) / (DH // 2))
    angles = query_pos.astype(F32)[:, None] * frequency[None, :]
    cosine = jnp.tile(jnp.cos(angles), (1, 4))
    sine = jnp.sin(angles)
    sine = jnp.concatenate([-sine, sine, -sine, sine], axis=1)
    here = jnp.stack([me, lax.axis_index("rep")]).astype(jnp.int32)
    place = (here, group, cosine, sine, bias)

    gains = flip_gather(jnp.stack([norm_attn[0], norm_ffn[0]]), count)
    gain_table = jnp.zeros((count,) + gains[0].shape, BF16)
    for p, piece in enumerate(gains):
        gain_table = lax.dynamic_update_slice(gain_table, piece[None], (me ^ p, 0, 0))
    gains = gain_table.transpose(1, 0, 2).reshape(2, 1, -1).astype(F32)
    qkv_shard = jnp.concatenate([w_query[0], w_key[0], w_value[0]], axis=1)
    weights = (
        row_pieces(qkv_shard, count),
        row_pieces(w_out[0], count),
        column_pieces(w_gate[0], count),
        column_pieces(w_up[0], count),
        row_pieces(w_down[0], count),
        gains[0],
        gains[1],
    )

    _, low, _ = forward_layer(given, weights, place, "a")
    received = shifted(low, "section", 1)
    layer_in = jnp.where(is_first, given, received)
    block, _, kept = forward_layer(layer_in, weights, place, "b")
    _, low, _, _ = backward_layer(given, kept, weights, place)
    received = shifted(low, "section", -1)
    out_grad = jnp.where(is_first, received, given)
    first_grad, _, pairs, gain_grads = backward_layer(out_grad, kept, weights, place)

    lefts = {k: left_rows(v[0], me, count, group) for k, v in pairs.items()}
    rights = {k: [right_rows(right, group) for right in v[1]] for k, v in pairs.items()}
    depths = {k: v[0].shape[1] // count for k, v in pairs.items()}
    gain_sums = jnp.concatenate(gain_grads, axis=0)
    for bit in bits_below(group):
        gain_sums = gain_sums + flip(gain_sums, bit)
    gain_sums = gain_sums.reshape(2, count, depths["q"]).transpose(1, 2, 0).astype(BF16)

    def chunk(name, part, row, rows, plane, col, cols, tile_cols, gained=False):
        k = name[0]
        other, own = grad_product(
            lefts[k], rights[k][part], depths[k], row, rows, plane, col, cols, tile_cols
        )
        if gained:
            other, own = with_gains(other, me ^ group), with_gains(own, me)
        return reduced(other, own, group)

    def with_gains(product, device):
        extra = lax.dynamic_index_in_dim(gain_sums, device, 0, keepdims=False)
        return jnp.concatenate([product, jnp.pad(extra, ((0, 0), (0, KT - 2)))], axis=1)

    model = half_width * 2
    half, depth = depths["d"] // 2, depths["g"]
    wide = w_gate.shape[2] // 2
    d_grad = [chunk(f"d{i}", 0, i * half, half, 0, 0, model, model // 3) for i in range(2)]
    gu_grad = [
        chunk(f"g{i}", 0, 0, depth, i // 2, (i % 2) * wide, wide, wide // 3) for i in range(4)
    ]
    o_grad = chunk("o", 0, 0, depths["o"], 0, 0, model, WK)
    q_grad = chunk("q", 0, 0, depths["q"], 0, 0, WQ, WK)
    kv_grad = chunk("qkv", 1, 0, depths["q"], 0, 0, 2 * WK, WK, True)

    def placed(result, from_first):
        kept_rows, sent_rows = result[:piece_rows], result[piece_rows:]
        back = flip(sent_rows.astype(BF16), group).astype(F32)
        first = jnp.where(micro == 0, kept_rows, back)
        second = jnp.where(micro == 0, back, kept_rows)
        rows = jnp.stack([first, second])
        low, high = rows[..., :half_width], rows[..., half_width:]
        if from_first:
            arrived = shifted(high.astype(BF16), "section", 1)
            return jnp.where(is_first, low, arrived.astype(F32))
        arrived = shifted(low.astype(BF16), "section", -1)
        return jnp.where(is_first, arrived.astype(F32), high)

    block_out = placed(block, False)[:, None]
    input_grad = placed(first_grad, True)[:, None]
    grads = [
        q_grad,
        kv_grad[:, :WK],
        kv_grad[:, WK : 2 * WK],
        o_grad,
        jnp.concatenate(gu_grad[:2], axis=1),
        jnp.concatenate(gu_grad[2:], axis=1),
        jnp.concatenate(d_grad, axis=0),
        kv_grad[:, 2 * WK],
        kv_grad[:, 2 * WK + 1],
    ]
    return (block_out, input_grad) + tuple(grad.astype(F32)[None] for grad in grads)


def solution(mesh):
    rows = P("section", "seq", None)
    tokens = P(None, "rep", "seq", "section")
    in_specs = (tokens,) + (rows,) * 7 + (P("section", "seq"),) * 2 + (P(None, "rep"), tokens)
    out_specs = (tokens, tokens) + (rows,) * 7 + (P("section", "seq"),) * 2

    return jax.shard_map(shards, mesh=mesh, in_specs=in_specs, out_specs=out_specs, check_vma=False)
```
